256 devices in a mesh: dp: 32 (over z, x_lo, core), shard: 8 (over y, x_hi).
Axes of the slice: x: 4 (x_hi: 2, x_lo: 2; x = x_hi * 2 + x_lo), y: 4, z: 8, core: 2. Of those that a mesh axis runs over, the one named last changes fastest.
Arguments:
- acts: bfloat16 [65536, 4096], P('dp', 'shard'), may hold values from -6 to 6
- grad_out: bfloat16 [65536, 14336], P('dp', 'shard'), may hold values from -15 to 15
- projector: bfloat16 [4096, 512], P('shard'), may hold values from -0.09375 to 0.09375
- weight: bfloat16 [4096, 14336], P('dp', 'shard'), may hold values from -0.09375 to 0.09375
- moment1: float32 [512, 14336], P('dp', 'shard'), may hold values from -24 to 24
- moment2: float32 [512, 14336], P('dp', 'shard'), may hold values from 1 to 16
Outputs:
- new_weight: bfloat16 [4096, 14336], P('dp', 'shard')
- new_moment1: float32 [512, 14336], P('dp', 'shard')
- new_moment2: float32 [512, 14336], P('dp', 'shard')
The draws below stay inside these ranges and needn't reach their ends.
All inputs are finite; a program needn't handle non-finite values.
Results may differ from the reference program's by a relative error of at most 0.005.
Values may be sent and summed in bfloat16 or wider, within the bound.
A program may use at most 64 MiB of HBM per device.

```python
import math
import jax
import jax.numpy as jnp

D = 4096
FF = 14336
R = 512
TOKENS = 65536


def draw_grad_out(key, part):
    key_noise, key_column = jax.random.split(key, 2)
    column = jnp.arange(FF, dtype=jnp.float32)
    column_scale = jnp.exp(jnp.log(3.0) * column / FF + jax.random.uniform(key_column, (FF,), jnp.float32, 0.0, jnp.log(10.0))) / 8.0
    base = jax.random.truncated_normal(key_noise, -4.0, 4.0, (TOKENS, FF), jnp.float32)
    return (base * column_scale).astype(jnp.bfloat16)


def level_of(stream_key, dims, cuts, smallest, high):
    def one(dim, blocks):
        heights = jax.random.uniform(jax.random.fold_in(jax.random.fold_in(stream_key, 6), dim), (blocks,), jnp.float32, smallest / len(cuts), high / len(cuts))
        return jnp.repeat(jnp.exp(heights), dims[dim] // blocks).reshape((-1,) + (1,) * (len(dims) - dim - 1))

    level = one(*cuts[0])
    for cut in cuts[1:]:
        level = level * one(*cut)
    return level


def centred(stream_key, dims, width, bound, cuts=(), held_as=jnp.bfloat16):
    entries = jax.random.normal(stream_key, dims, jnp.float32) * width
    if len(cuts) > 0:
        entries = level_of(stream_key, dims, cuts, -0.22, 0.18) * entries
    return jnp.clip(entries, min=-bound, max=bound).astype(held_as)


def setup_inputs(seed: int = 0) -> dict:
    seeds = jax.random.split(jax.random.key(seed), 7)
    acts = centred(seeds[0], (TOKENS, D), 1.0, 6.0, ((0, 32), (1, 8)))
    grad_out = draw_grad_out(jax.random.fold_in(seeds[6], 71), 0)
    projector = centred(seeds[2], (D, R), D ** -0.5, 0.09375, ((0, 8),))
    weight = centred(seeds[3], (D, FF), D ** -0.5, 0.09375, ((0, 32), (1, 8)))
    moment1 = centred(seeds[4], (R, FF), 4.0, 24.0, ((0, 32), (1, 8)), jnp.float32)
    moment2 = jnp.clip(jnp.exp(math.log(16.0) - 2.7725887 * jax.random.uniform(seeds[5], (R, FF), jnp.float32) ** level_of(seeds[5], (R, FF), ((0, 32), (1, 8)), -0.2, 0.2)), 1.0, 16.0)
    return dict(acts=acts, grad_out=grad_out, projector=projector, weight=weight, moment1=moment1, moment2=moment2)


first_fix = 0.9999734386011124
second_fix = 0.994079470779666

def reference(acts, grad_out, projector, weight, moment1, moment2):
    projected = jnp.dot(acts, projector, preferred_element_type=jnp.float32).astype(jnp.bfloat16)
    gradient = jnp.dot(projected.T, grad_out, preferred_element_type=jnp.float32)
    root_mean = jnp.sqrt(jnp.sum(gradient * gradient) / (R * FF) + 1e-06)
    clip_factor = jnp.minimum(1.0, 4.0 / root_mean)
    clipped = clip_factor * gradient
    new_moment1 = 0.9 * moment1 + 0.1 * clipped
    new_moment2 = 0.95 * moment2 + 0.05 * clipped * clipped
    update = (new_moment1 / first_fix / (jnp.sqrt(new_moment2 / second_fix) + 1e-08)).astype(jnp.bfloat16)
    change = jnp.dot(projector, update, preferred_element_type=jnp.float32)
    new_weight = (weight.astype(jnp.float32) - 0.2 * change).astype(jnp.bfloat16)
    return (new_weight, new_moment1, new_moment2)
```

```python
import functools

import jax
import jax.numpy as jnp
from jax import lax
from jax.experimental import pallas as pl
from jax.experimental.pallas import tpu as pltpu
from jax.sharding import Mesh
from jax.sharding import PartitionSpec as P

MESH = pl.DeviceIdType.MESH
TOKENS = 2048
FEATS = 512
R = 512
COLS = 1792
FF = 14336
BLOCKS = 4
RANKS = R // BLOCKS
PIECE = 128
ROWS = 16
TILE = 256
OFFSETS = (('project', 0), ('chain', 1), ('second', 5), ('third', 8), ('fourth', 12), ('forward', 13), ('multiply', 16), ('along_z', 19), ('along_x', 27))
PERIOD = 3
CHAINED = ()
FORWARDED = ()
SIZES = {"z": 8, "xl": 2, "c": 2, "y": 4, "xh": 2}
FAR_FIRST = (4, 3, 5, 2, 6, 1, 7)

first_fix = 0.9999734386011124
second_fix = 0.994079470779666


def f32(x):
    return x.astype(jnp.float32)


def bf16(x):
    return x.astype(jnp.bfloat16)


class Copies:
    def __init__(self, send_sems, recv_sems):
        self.send_sems, self.recv_sems, self.count = send_sems, recv_sems, 0

    def next(self):
        self.count += 1
        return self.count - 1

    def make(self, src, dst, recv=None, **device):
        k = self.next()
        return pltpu.make_async_remote_copy(
            src_ref=src,
            dst_ref=dst,
            send_sem=self.send_sems.at[k],
            recv_sem=self.recv_sems.at[k if recv is None else recv],
            device_id=device,
            device_id_type=MESH,
        )


def kernel(
    acts_h, grad_h, proj_h, weight_h, m1_h, m2_h,
    w_o, m1_o, m2_o,
    acts, grad, proj, proj_t, weight, m1, m2,
    s1, q1, r1, x1s, x1r, s2, r2, y2s, y2r, full,
    mine, core_s, core_r, z_s, z_own, z_r, x_s, x_r,
    sq, sq_z, sq_s, sq_c, upd, basis, new_w, new_m1, new_m2,
    send_sems, recv_sems, local_sems,
):
    z, xl, c = lax.axis_index("z"), lax.axis_index("xl"), lax.axis_index("c")
    y, xh = lax.axis_index("y"), lax.axis_index("xh")
    shard = y * 2 + xh
    me = {"z": z, "xl": xl, "c": c, "y": y, "xh": xh}

    def at(axis, step):
        return lax.rem(me[axis] + step, SIZES[axis])

    def shard_at(step):
        other = lax.rem(shard + step, 8)
        return {"y": lax.div(other, 2), "xh": lax.rem(other, 2)}

    loads = {}
    for k, (name, src, dst) in enumerate(
        (
            ("proj", proj_h, proj),
            ("acts", acts_h, acts),
            ("grad", grad_h, grad),
            ("m1", m1_h, m1),
            ("m2", m2_h, m2),
            ("weight", weight_h, weight),
        )
    ):
        loads[name] = pltpu.make_async_copy(src, dst, local_sems.at[k])
    loads["proj"].start()
    loads["acts"].start()

    partners = [{"z": at("z", d)} for d in range(1, 8)]
    partners += [shard_at(d) for d in range(1, 8)]
    partners += [{"c": 1 - c}, {"xl": 1 - xl}]
    barrier = pltpu.get_barrier_semaphore()
    for partner in partners:
        pl.semaphore_signal(barrier, inc=1, device_id=partner, device_id_type=MESH)

    loads["proj"].wait()
    proj_t[...] = proj[...].T
    loads["acts"].wait()
    for name in ("grad", "m1", "m2", "weight"):
        loads[name].start()

    copies = Copies(send_sems, recv_sems)
    sent = []

    def start(copy):
        copy.start()
        sent.append(copy)
        return copy

    def ranks_of(b):
        return jnp.concatenate(
            [proj_t[pl.ds(64 * k + ROWS * b, ROWS), :] for k in range(8)], axis=0
        )

    def project(lhs, token, count):
        rows = acts[pl.ds(pl.multiple_of(token, PIECE), count), :]
        return bf16(
            lax.dot_general(
                lhs, rows, (((1,), (1,)), ((), ())), preferred_element_type=jnp.float32
            )
        )

    st = [dict() for _ in range(BLOCKS)]

    def stage1(b):
        lhs = ranks_of(b)

        def x_half(h):
            token = 1024 + lax.rem(xh + h, 2) * 512
            out = project(lhs, token, 512)
            for k in range(4):
                s2[b, h, k] = out[:, k * PIECE : (k + 1) * PIECE]

        def y_quarter(d):
            out = project(lhs, at("y", d) * 256, 256)
            for k in range(2):
                s1[b, d, k] = out[:, k * PIECE : (k + 1) * PIECE]

        x_half(1)
        if b == 0:
            pl.semaphore_wait(barrier, len(partners))
        st[b]["r2"] = start(copies.make(s2.at[b, 1], r2.at[b], xh=1 - xh))
        y_quarter(2)
        if b in CHAINED:
            st[b]["q1"] = [
                start(copies.make(s1.at[b, 2, k], q1.at[b, k], y=at("y", d)))
                for k, d in enumerate((1, 3))
            ]
            y_quarter(1)
            y_quarter(3)
        else:
            st[b]["r1"] = [start(copies.make(s1.at[b, 2], r1.at[b, 2], y=at("y", 2)))]
            for k, d in enumerate((1, 3)):
                y_quarter(d)
                st[b]["r1"].append(
                    start(copies.make(s1.at[b, d], r1.at[b, k], y=at("y", d)))
                )
        x_half(0)
        y_quarter(0)

    def chain(b):
        if b not in CHAINED:
            return
        st[b]["r1"] = []
        for k, d in enumerate((1, 3)):
            st[b]["q1"][k].wait_recv()
            s1[b, d, k] = bf16(f32(s1[b, d, k]) + f32(q1[b, k]))
            st[b]["r1"].append(
                start(copies.make(s1.at[b, d], r1.at[b, k], y=at("y", d)))
            )

    def sum1(b, half):
        value = f32(s1[b, 0, half]) + f32(r1[b, 0, half]) + f32(r1[b, 1, half])
        return value if b in CHAINED else value + f32(r1[b, 2, half])

    def stage2(b):
        for copy in st[b]["r1"]:
            copy.wait_recv()
        x1s[b] = bf16(sum1(b, 1 - xh))
        st[b]["x1"] = start(copies.make(x1s.at[b], x1r.at[b], xh=1 - xh))
        st[b]["r2"].wait_recv()
        st[b]["y2"] = []
        for d in (2, 1, 3):
            other = at("y", d)
            y2s[b, d - 1] = bf16(f32(s2[b, 0, other]) + f32(r2[b, other]))
            st[b]["y2"].append(
                start(copies.make(y2s.at[b, d - 1], y2r.at[b, d - 1], y=other))
            )

    def stage3(b):
        st[b]["x1"].wait_recv()
        slot = 8 * b + y * 2 + xh
        full[0, slot] = bf16(sum1(b, xh) + f32(x1r[b]))
        st[b]["x3"] = start(copies.make(full.at[0, slot], full.at[0, slot], xh=1 - xh))
        for copy in st[b]["y2"]:
            copy.wait_recv()
        value = f32(s2[b, 0, y]) + f32(r2[b, y])
        for k in range(3):
            value += f32(y2r[b, k])
        slot = 8 * b + xh * 4 + y
        full[1, slot] = bf16(value)
        st[b]["y3"] = [
            start(copies.make(full.at[1, slot], full.at[1, slot], y=at("y", d)))
            for d in (2, 1, 3)
        ]

    def stage4(b):
        st[b]["x3"].wait_recv()
        pair = full.at[0, pl.ds(8 * b + y * 2, 2)]
        steps = (1, 3) if b in FORWARDED else (1, 3, 2)
        st[b]["y4"] = [start(copies.make(pair, pair, y=at("y", d))) for d in steps]
        for copy in st[b]["y3"]:
            copy.wait_recv()
        four = full.at[1, pl.ds(8 * b + xh * 4, 4)]
        st[b]["x4"] = start(copies.make(four, four, xh=1 - xh))

    def forward(b):
        if b not in FORWARDED:
            st[b]["y5"] = st[b]["y4"]
            return
        st[b]["y5"] = []
        for k, d in enumerate((1, 3)):
            st[b]["y4"][k].wait_recv()
            one = full.at[0, 8 * b + at("y", 4 - d) * 2 + k]
            st[b]["y5"].append(start(copies.make(one, one, y=at("y", d))))

    def parts(b):
        return ((0, 4), (4, 7)) if b == BLOCKS - 1 else ((0, 7),)

    def multiply(b):
        for copy in st[b]["y5"]:
            copy.wait_recv()
        st[b]["x4"].wait_recv()
        if b == 0:
            loads["grad"].wait()
        near = c == b % 2
        st[b]["near"] = near
        st[b]["core"] = []

        def columns(n, carry):
            here = pl.ds(pl.multiple_of(n * TILE, TILE), TILE)
            lhs = jnp.concatenate(
                [full[part, 8 * b + k] for part in range(2) for k in range(8)], axis=1
            )
            out = jnp.dot(lhs, grad[:, here], preferred_element_type=jnp.float32)

            @pl.when(near)
            def _():
                mine[b // 2, :, here] = out

            @pl.when(jnp.logical_not(near))
            def _():
                for k in range(8):
                    core_s[b, k, :, here] = bf16(out[k * ROWS : (k + 1) * ROWS])

            return carry

        for low, high in parts(b):
            span = pl.ds(low * TILE, (high - low) * TILE)
            copy = copies.make(core_s.at[b, :, :, span], core_r.at[b, :, :, span], c=1 - c)
            st[b]["core"].append(copy)
            lax.fori_loop(low, high, columns, 0)
            pl.when(jnp.logical_not(near))(copy.start)

    def along_z(b):
        j = b // 2
        st[b]["z"] = []
        for low, high in parts(b):
            span = pl.ds(low * TILE, (high - low) * TILE)
            st[b]["z"].append(
                [
                    copies.make(
                        z_s.at[j, at("z", d), :, span], z_r.at[j, d - 1, :, span], z=at("z", d)
                    )
                    for d in FAR_FIRST
                ]
            )

        @pl.when(st[b]["near"])
        def _():
            for (low, high), core, group in zip(parts(b), st[b]["core"], st[b]["z"]):
                span = slice(low * TILE, high * TILE)
                core.wait_recv()
                for k in range(8):
                    z_s[j, k, :, span] = bf16(
                        mine[j, k * ROWS : (k + 1) * ROWS, span] + f32(core_r[b, k, :, span])
                    )
                for copy in group:
                    copy.start()
                own = pl.ds(pl.multiple_of(z * ROWS, ROWS), ROWS)
                z_own[j, :, span] = mine[j, own, span] + f32(core_r[b, z, :, span])

    def along_x(b):
        j = b // 2
        spans = [pl.ds(low * TILE, (high - low) * TILE) for low, high in parts(b)]
        st[b]["x"] = [
            copies.make(x_s.at[j, :, span], x_r.at[j, :, span], xl=1 - xl) for span in spans
        ]

        @pl.when(st[b]["near"])
        def _():
            for (low, high), group, copy in zip(parts(b), st[b]["z"], st[b]["x"]):
                span = slice(low * TILE, high * TILE)
                for arrived in group:
                    arrived.wait_recv()
                value = z_own[j, :, span]
                for k in range(7):
                    value += f32(z_r[j, k, :, span])
                z_own[j, :, span] = value
                x_s[j, :, span] = bf16(value)
                copy.start()

    offset = pl.multiple_of((xl * 2 + c) * PIECE, PIECE)
    rows = proj.at[pl.ds(offset, PIECE)]
    basis_sem = copies.next()
    to_basis = [copies.make(rows, basis, recv=basis_sem, **shard_at(d)) for d in range(1, 8)]

    def send_basis():
        @pl.when(shard == z)
        def _():
            for copy in to_basis:
                copy.start()
            basis[...] = proj[pl.ds(offset, PIECE), :]

    stages = {
        "project": stage1, "chain": chain, "second": stage2, "third": stage3, "fourth": stage4,
        "forward": forward, "multiply": multiply, "along_z": along_z, "along_x": along_x,
    }
    order = sorted(
        (b * PERIOD + offset, b, name) for b in range(BLOCKS) for name, offset in OFFSETS
    )
    for _, b, name in order:
        stages[name](b)
        if (name, b) == ("multiply", BLOCKS - 1):
            send_basis()

    for b in range(BLOCKS):

        @pl.when(st[b]["near"])
        def _():
            for copy in st[b]["x"]:
                copy.wait_recv()

    value = jnp.zeros((8, 128), jnp.float32)
    for j in range(2):
        gradient = z_own[j] + f32(x_r[j])
        z_own[j] = gradient
        square = gradient * gradient
        square = square[:8] + square[8:]
        for k in range(COLS // 128):
            value += square[:, k * 128 : (k + 1) * 128]

    def exchange(value, step, slots, partners):
        sq[step] = value
        arriving = [
            start(copies.make(sq.at[step], slots.at[k], **partner))
            for k, partner in enumerate(partners)
        ]
        for k, copy in enumerate(arriving):
            copy.wait_recv()
            value += slots[k]
        return value

    value = exchange(value, 0, sq_c, [{"c": 1 - c}])
    value = exchange(value, 1, sq_s, [shard_at(d) for d in range(1, 8)])
    value = exchange(value, 2, sq_z, [{"z": at("z", d)} for d in FAR_FIRST])
    root_mean = jnp.sqrt(jnp.sum(value, keepdims=True) / (R * FF) + 1e-06)
    clip_factor = jnp.minimum(1.0, 4.0 / root_mean)

    for name in ("m1", "m2", "weight"):
        loads[name].wait()
    clipped = clip_factor * z_own[xl]
    moment1 = 0.9 * m1[...] + 0.1 * clipped
    moment2 = 0.95 * m2[...] + 0.05 * clipped * clipped
    upd[z, xl, c] = bf16(moment1 / first_fix / (jnp.sqrt(moment2 / second_fix) + 1e-08))

    def piece(zz, xx):
        return upd.at[zz, xx, c]

    across, last = {}, []

    def z_copy(part, step):
        return start(copies.make(part, part, z=at("z", step)))

    def pass_on(zz, key):
        across[key] = start(copies.make(piece(zz, xl), piece(zz, xl), xl=1 - xl))
        last.append(start(copies.make(piece(zz, xl), piece(zz, xl), c=1 - c)))

    def pass_core(zz, key):
        across[key].wait_recv()
        last.append(start(copies.make(piece(zz, 1 - xl), piece(zz, 1 - xl), c=1 - c)))

    coming = {step: z_copy(piece(z, xl), step) for step in (1, 7)}
    pass_on(z, 0)
    new_m1[...] = moment1
    new_m2[...] = moment2
    stores = [
        pltpu.make_async_copy(new_m1, m1_o, local_sems.at[6]),
        pltpu.make_async_copy(new_m2, m2_o, local_sems.at[7]),
    ]
    for store in stores:
        store.start()
    waiting = [(z, 0)]
    for hop in (1, 2, 3):
        arrived, coming = coming, {}
        for step in (1, 7):
            arrived[step].wait_recv()
            zz = at("z", hop * (8 - step))
            part = piece(zz, xl)
            if hop == 3:
                part = upd.at[zz, xl, c, :, pl.ds(0 if step == 1 else COLS // 2, COLS // 2)]
            coming[step] = z_copy(part, step)
            pass_on(zz, (hop, step))
            waiting.append((zz, (hop, step)))
        while len(waiting) > 2:
            pass_core(*waiting.pop(0))
    for step in (1, 7):
        coming[step].wait_recv()
    pass_on(at("z", 4), 4)
    waiting.append((at("z", 4), 4))
    for item in waiting:
        pass_core(*item)

    @pl.when(shard != z)
    def _():
        to_basis[0].wait_recv()

    for copy in last:
        copy.wait_recv()

    def out_columns(n, carry):
        here = pl.ds(pl.multiple_of(n * TILE, TILE), TILE)
        rows = jnp.concatenate(
            [upd[k // 4, (k // 2) % 2, k % 2, :, here] for k in range(32)], axis=0
        )
        change = jnp.dot(basis[...], rows, preferred_element_type=jnp.float32)
        new_w[:, here] = bf16(f32(weight[:, here]) - 0.2 * change)
        return carry

    lax.fori_loop(0, COLS // TILE, out_columns, 0)
    stores.append(pltpu.make_async_copy(new_w, w_o, local_sems.at[8]))
    stores[-1].start()

    assert copies.count <= SEMS
    for copy in sent:
        copy.wait_send()
    for b in range(BLOCKS):

        @pl.when(st[b]["near"])
        def _():
            for group in (*st[b]["z"], st[b]["x"]):
                for copy in group:
                    copy.wait_send()

        @pl.when(jnp.logical_not(st[b]["near"]))
        def _():
            for copy in st[b]["core"]:
                copy.wait_send()

    @pl.when(shard == z)
    def _():
        for copy in to_basis:
            copy.wait_send()

    for store in stores:
        store.wait()


def handed_on(w, m1, m2, w_o, m1_o, m2_o):
    w_o[...], m1_o[...], m2_o[...] = w[...], m1[...], m2[...]


SEMS = 224


def step(acts, grad_out, projector, weight, moment1, moment2):
    hbm = pl.BlockSpec(memory_space=pltpu.MemorySpace.HBM)
    half, full = jnp.bfloat16, jnp.float32
    pieces = (RANKS, PIECE)
    owned = (ROWS, COLS)
    scratch = [
        pltpu.VMEM(acts.shape, half),
        pltpu.VMEM(grad_out.shape, half),
        pltpu.VMEM(projector.shape, half),
        pltpu.VMEM(projector.shape, half),
        pltpu.VMEM(weight.shape, half),
        pltpu.VMEM(owned, full),
        pltpu.VMEM(owned, full),
        pltpu.VMEM((BLOCKS, 4, 2, *pieces), half),
        pltpu.VMEM((BLOCKS, 2, *pieces), half),
        pltpu.VMEM((BLOCKS, 3, 2, *pieces), half),
        pltpu.VMEM((BLOCKS, *pieces), half),
        pltpu.VMEM((BLOCKS, *pieces), half),
        pltpu.VMEM((BLOCKS, 2, 4, *pieces), half),
        pltpu.VMEM((BLOCKS, 4, *pieces), half),
        pltpu.VMEM((BLOCKS, 3, *pieces), half),
        pltpu.VMEM((BLOCKS, 3, *pieces), half),
        pltpu.VMEM((2, BLOCKS * 8, *pieces), half),
        pltpu.VMEM((2, RANKS, COLS), full),
        pltpu.VMEM((BLOCKS, 8, *owned), half),
        pltpu.VMEM((BLOCKS, 8, *owned), half),
        pltpu.VMEM((2, 8, *owned), half),
        pltpu.VMEM((2, *owned), full),
        pltpu.VMEM((2, 7, *owned), half),
        pltpu.VMEM((2, *owned), half),
        pltpu.VMEM((2, *owned), half),
        pltpu.VMEM((3, 8, 128), full),
        pltpu.VMEM((7, 8, 128), full),
        pltpu.VMEM((7, 8, 128), full),
        pltpu.VMEM((1, 8, 128), full),
        pltpu.VMEM((8, 2, 2, *owned), half),
        pltpu.VMEM((PIECE, R), half),
        pltpu.VMEM(weight.shape, half),
        pltpu.VMEM(owned, full),
        pltpu.VMEM(owned, full),
        pltpu.SemaphoreType.DMA((SEMS,)),
        pltpu.SemaphoreType.DMA((SEMS,)),
        pltpu.SemaphoreType.DMA((9,)),
    ]
    outs = (
        jax.ShapeDtypeStruct(weight.shape, half),
        jax.ShapeDtypeStruct(owned, full),
        jax.ShapeDtypeStruct(owned, full),
    )
    results = pl.pallas_call(
        kernel,
        out_shape=outs,
        in_specs=[hbm] * 6,
        out_specs=(hbm,) * 3,
        scratch_shapes=scratch,
        name="galore_step",
        compiler_params=pltpu.CompilerParams(
            collective_id=0, has_side_effects=True, vmem_limit_bytes=56 << 20
        ),
    )(acts, grad_out, projector, weight, moment1, moment2)
    return pl.pallas_call(
        handed_on,
        out_shape=outs,
        name="handed_on",
    )(*results)


def solution(mesh):
    finer = Mesh(mesh.devices.reshape(8, 2, 2, 4, 2), ("z", "xl", "c", "y", "xh"))
    dp, shard = ("z", "xl", "c"), ("y", "xh")
    both = P(dp, shard)
    return jax.shard_map(
        step,
        mesh=finer,
        in_specs=(both, both, P(shard, None), both, both, both),
        out_specs=(both, both, both),
        check_vma=False,
    )
```

```python
import functools

import jax
import jax.numpy as jnp
from jax import lax
from jax.experimental import pallas as pl
from jax.experimental.pallas import tpu as pltpu
from jax.sharding import Mesh
from jax.sharding import PartitionSpec as P

MESH = pl.DeviceIdType.MESH
TOKENS = 2048
FEATS = 512
R = 512
COLS = 1792
FF = 14336
BLOCKS = 4
RANKS = R // BLOCKS
PIECE = 128
ROWS = 16
TILE = 896
OFFSETS = dict(p=0, sx=5, sy=4.9, tx=8, ty=7.9, fy=12, fx=11.9, m=16, n=16.1, o=16.2, z=19, x=27)
PERIOD = 3
ORDER = [
    (name, b)
    for _, b, name in sorted(
        (b * PERIOD + offset, b, name) for b in range(BLOCKS) for name, offset in OFFSETS.items()
    )
]
FIRST_PRODUCT = next(item for item in ORDER if item[0] == "m")
SIZES = {"z": 8, "xl": 2, "c": 2, "y": 4, "xh": 2}
FAR_FIRST = (4, 3, 5, 2, 6, 1, 7)

first_fix = 0.9999734386011124
second_fix = 0.994079470779666


def f32(x):
    return x.astype(jnp.float32)


def bf16(x):
    return x.astype(jnp.bfloat16)


class Copies:
    def __init__(self, send_sems, recv_sems):
        self.send_sems, self.recv_sems, self.count = send_sems, recv_sems, 0

    def next(self):
        self.count += 1
        return self.count - 1

    def make(self, src, dst, recv=None, **device):
        k = self.next()
        return pltpu.make_async_remote_copy(
            src_ref=src,
            dst_ref=dst,
            send_sem=self.send_sems.at[k],
            recv_sem=self.recv_sems.at[k if recv is None else recv],
            device_id=device,
            device_id_type=MESH,
        )


def kernel(
    acts_h, grad_h, proj_h, weight_h, m1_h, m2_h,
    w_o, m1_o, m2_o,
    acts, grad, proj, proj_t, weight, m1, m2,
    s1, r1, x1s, x1r, s2, r2, y2s, y2r, full,
    mine, core_s, core_r, z_s, z_own, z_r, x_s, x_r,
    sq, sq_z, sq_s, sq_c, upd, basis,
    send_sems, recv_sems, local_sems,
):
    z, xl, c = lax.axis_index("z"), lax.axis_index("xl"), lax.axis_index("c")
    y, xh = lax.axis_index("y"), lax.axis_index("xh")
    shard = y * 2 + xh
    me = {"z": z, "xl": xl, "c": c, "y": y, "xh": xh}

    def at(axis, step):
        return lax.rem(me[axis] + step, SIZES[axis])

    def shard_at(step):
        other = lax.rem(shard + step, 8)
        return {"y": lax.div(other, 2), "xh": lax.rem(other, 2)}

    loads = {}
    for k, (name, src, dst) in enumerate(
        (
            ("proj", proj_h, proj),
            ("acts", acts_h, acts),
            ("grad", grad_h, grad),
            ("m1", m1_h, m1),
            ("m2", m2_h, m2),
            ("weight", weight_h, weight),
        )
    ):
        loads[name] = pltpu.make_async_copy(src, dst, local_sems.at[k])
    loads["proj"].start()
    loads["acts"].start()

    partners = [{"z": at("z", d)} for d in range(1, 8)]
    partners += [shard_at(d) for d in range(1, 8)]
    partners += [{"c": 1 - c}, {"xl": 1 - xl}]
    barrier = pltpu.get_barrier_semaphore()
    for partner in partners:
        pl.semaphore_signal(barrier, inc=1, device_id=partner, device_id_type=MESH)

    loads["proj"].wait()
    proj_t[...] = proj[...].T
    loads["acts"].wait()
    for name in ("grad", "m1", "m2", "weight"):
        loads[name].start()

    copies = Copies(send_sems, recv_sems)
    sent = []

    def start(copy):
        copy.start()
        sent.append(copy)
        return copy

    def ranks_of(b):
        return jnp.concatenate(
            [proj_t[pl.ds(64 * k + ROWS * b, ROWS), :] for k in range(8)], axis=0
        )

    def project(lhs, token, count):
        rows = acts[pl.ds(pl.multiple_of(token, PIECE), count), :]
        return bf16(
            lax.dot_general(
                lhs, rows, (((1,), (1,)), ((), ())), preferred_element_type=jnp.float32
            )
        )

    st = [dict() for _ in range(BLOCKS)]

    def project_block(b):
        lhs = ranks_of(b)

        def x_half(h):
            token = 1024 + lax.rem(xh + h, 2) * 512
            out = project(lhs, token, 512)
            for k in range(4):
                s2[b, h, k] = out[:, k * PIECE : (k + 1) * PIECE]

        def y_quarter(d):
            out = project(lhs, at("y", d) * 256, 256)
            for k in range(2):
                s1[b, d, k] = out[:, k * PIECE : (k + 1) * PIECE]

        x_half(1)
        if b == ORDER[0][1]:
            pl.semaphore_wait(barrier, len(partners))
        st[b]["r2"] = start(copies.make(s2.at[b, 1], r2.at[b], xh=1 - xh))
        y_quarter(2)
        st[b]["r1"] = [start(copies.make(s1.at[b, 2], r1.at[b, 2], y=at("y", 2)))]
        for k, d in enumerate((1, 3)):
            y_quarter(d)
            st[b]["r1"].append(start(copies.make(s1.at[b, d], r1.at[b, k], y=at("y", d))))
        x_half(0)
        y_quarter(0)

    def sum1(b, half):
        value = f32(s1[b, 0, half])
        for k in range(3):
            value += f32(r1[b, k, half])
        return value

    def second_x(b):
        for copy in st[b]["r1"]:
            copy.wait_recv()
        x1s[b] = bf16(sum1(b, 1 - xh))
        st[b]["x1"] = start(copies.make(x1s.at[b], x1r.at[b], xh=1 - xh))

    def second_y(b):
        st[b]["r2"].wait_recv()
        st[b]["y2"] = []
        for d in (2, 1, 3):
            other = at("y", d)
            y2s[b, d - 1] = bf16(f32(s2[b, 0, other]) + f32(r2[b, other]))
            st[b]["y2"].append(
                start(copies.make(y2s.at[b, d - 1], y2r.at[b, d - 1], y=other))
            )

    def third_x(b):
        st[b]["x1"].wait_recv()
        slot = 8 * b + y * 2 + xh
        full[0, slot] = bf16(sum1(b, xh) + f32(x1r[b]))
        st[b]["x3"] = start(copies.make(full.at[0, slot], full.at[0, slot], xh=1 - xh))

    def third_y(b):
        for copy in st[b]["y2"]:
            copy.wait_recv()
        value = f32(s2[b, 0, y]) + f32(r2[b, y])
        for k in range(3):
            value += f32(y2r[b, k])
        slot = 8 * b + xh * 4 + y
        full[1, slot] = bf16(value)
        st[b]["y3"] = [
            start(copies.make(full.at[1, slot], full.at[1, slot], y=at("y", d)))
            for d in (2, 1, 3)
        ]

    def fourth_y(b):
        st[b]["x3"].wait_recv()
        pair = full.at[0, pl.ds(8 * b + y * 2, 2)]
        st[b]["y4"] = [start(copies.make(pair, pair, y=at("y", d))) for d in (1, 3, 2)]

    def fourth_x(b):
        for copy in st[b]["y3"]:
            copy.wait_recv()
        four = full.at[1, pl.ds(8 * b + xh * 4, 4)]
        st[b]["x4"] = start(copies.make(four, four, xh=1 - xh))

    def parts(b):
        return ((0, 1), (1, 2)) if b == BLOCKS - 1 else ((0, 2),)

    def span_of(part):
        return pl.ds(part[0] * TILE, (part[1] - part[0]) * TILE)

    def arrived(b):
        for copy in st[b]["y4"]:
            copy.wait_recv()
        st[b]["x4"].wait_recv()
        st[b]["near"] = c == b % 2
        st[b]["core"] = []
        for part in parts(b):
            span = span_of(part)
            st[b]["core"].append(
                copies.make(core_s.at[b, :, :, span], core_r.at[b, :, :, span], c=1 - c)
            )

    def multiply(b, low, high):
        near = st[b]["near"]

        def columns(n, carry):
            here = pl.ds(pl.multiple_of(n * TILE, TILE), TILE)
            lhs = jnp.concatenate(
                [full[part, 8 * b + k] for part in range(2) for k in range(8)], axis=1
            )
            out = jnp.dot(lhs, grad[:, here], preferred_element_type=jnp.float32)

            @pl.when(near)
            def _():
                mine[b // 2, :, here] = out

            @pl.when(jnp.logical_not(near))
            def _():
                for k in range(8):
                    core_s[b, k, :, here] = bf16(out[k * ROWS : (k + 1) * ROWS])

            return carry

        lax.fori_loop(low, high, columns, 0)

    def multiply_0(b):
        arrived(b)
        pass

    def multiply_1(b):
        multiply(b, 0, 1)
        if len(parts(b)) > 1:
            pl.when(jnp.logical_not(st[b]["near"]))(st[b]["core"][0].start)

    def multiply_2(b):
        multiply(b, 1, 2)
        pl.when(jnp.logical_not(st[b]["near"]))(st[b]["core"][-1].start)

    def along_z(b):
        j = b // 2
        st[b]["z"] = []
        for part in parts(b):
            span = span_of(part)
            st[b]["z"].append(
                [
                    copies.make(
                        z_s.at[j, at("z", d), :, span], z_r.at[j, d - 1, :, span], z=at("z", d)
                    )
                    for d in FAR_FIRST
                ]
            )

        @pl.when(st[b]["near"])
        def _():
            for (low, high), core, group in zip(parts(b), st[b]["core"], st[b]["z"]):
                span = slice(low * TILE, high * TILE)
                core.wait_recv()
                for k in range(8):
                    z_s[j, k, :, span] = bf16(
                        mine[j, k * ROWS : (k + 1) * ROWS, span] + f32(core_r[b, k, :, span])
                    )
                for copy in group:
                    copy.start()
                own = pl.ds(pl.multiple_of(z * ROWS, ROWS), ROWS)
                z_own[j, :, span] = mine[j, own, span] + f32(core_r[b, z, :, span])

    def along_x(b):
        j = b // 2
        spans = [span_of(part) for part in parts(b)]
        st[b]["x"] = [
            copies.make(x_s.at[j, :, span], x_r.at[j, :, span], xl=1 - xl) for span in spans
        ]

        @pl.when(st[b]["near"])
        def _():
            for (low, high), group, copy in zip(parts(b), st[b]["z"], st[b]["x"]):
                span = slice(low * TILE, high * TILE)
                for arrived in group:
                    arrived.wait_recv()
                value = z_own[j, :, span]
                for k in range(7):
                    value += f32(z_r[j, k, :, span])
                z_own[j, :, span] = value
                x_s[j, :, span] = bf16(value)
                copy.start()

    offset = pl.multiple_of((xl * 2 + c) * PIECE, PIECE)
    rows = proj.at[pl.ds(offset, PIECE)]
    basis_sem = copies.next()
    to_basis = [copies.make(rows, basis, recv=basis_sem, **shard_at(d)) for d in range(1, 8)]

    def send_basis():
        @pl.when(shard == z)
        def _():
            for copy in to_basis:
                copy.start()
            basis[...] = proj[pl.ds(offset, PIECE), :]

    stages = {
        "p": project_block, "sx": second_x, "sy": second_y, "tx": third_x, "ty": third_y,
        "fy": fourth_y, "fx": fourth_x, "m": multiply_0, "n": multiply_1, "o": multiply_2,
        "z": along_z, "x": along_x,
    }
    for name, b in ORDER:
        if (name, b) == FIRST_PRODUCT:
            loads["grad"].wait()
        stages[name](b)
        if (name, b) == ("o", BLOCKS - 1):
            send_basis()

    for b in range(BLOCKS):

        @pl.when(st[b]["near"])
        def _():
            for copy in st[b]["x"]:
                copy.wait_recv()

    value = jnp.zeros((8, 128), jnp.float32)
    for j in range(2):
        gradient = z_own[j] + f32(x_r[j])
        z_own[j] = gradient
        square = gradient * gradient
        square = square[:8] + square[8:]
        for k in range(COLS // 128):
            value += square[:, k * 128 : (k + 1) * 128]

    def exchange(value, step, slots, partners):
        sq[step] = value
        arriving = [
            start(copies.make(sq.at[step], slots.at[k], **partner))
            for k, partner in enumerate(partners)
        ]
        for k, copy in enumerate(arriving):
            copy.wait_recv()
            value += slots[k]
        return value

    value = exchange(value, 0, sq_c, [{"c": 1 - c}])
    value = exchange(value, 1, sq_s, [shard_at(d) for d in range(1, 8)])
    value = exchange(value, 2, sq_z, [{"z": at("z", d)} for d in FAR_FIRST])
    root_mean = jnp.sqrt(jnp.sum(value, keepdims=True) / (R * FF) + 1e-06)
    clip_factor = jnp.minimum(1.0, 4.0 / root_mean)

    for name in ("m1", "m2", "weight"):
        loads[name].wait()
    clipped = clip_factor * z_own[xl]
    moment1 = 0.9 * m1[...] + 0.1 * clipped
    moment2 = 0.95 * m2[...] + 0.05 * clipped * clipped
    upd[z, xl, c] = bf16(moment1 / first_fix / (jnp.sqrt(moment2 / second_fix) + 1e-08))

    def piece(zz, xx):
        return upd.at[zz, xx, c]

    across, last = [], []

    def z_copy(part, step):
        return start(copies.make(part, part, z=at("z", step)))

    halves = [pl.ds(k * (COLS // 2), COLS // 2) for k in range(2)]

    def pass_on(step, k=None):
        zz = at("z", step)
        span = slice(None) if k is None else halves[k]
        part = upd.at[zz, xl, c, :, span]
        other = upd.at[zz, 1 - xl, c, :, span]
        across.append((start(copies.make(part, part, xl=1 - xl)), other))
        last.append(start(copies.make(part, part, c=1 - c)))

    def pass_core(keep):
        while len(across) > keep:
            copy, other = across.pop(0)
            copy.wait_recv()
            last.append(start(copies.make(other, other, c=1 - c)))

    coming = {}
    for k in range(2):
        for step in (1, 7):
            coming[step, k] = z_copy(upd.at[z, xl, c, :, halves[k]], step)
    opposite = z_copy(piece(z, xl), 4)
    pass_on(0)
    m1_o[...] = moment1
    m2_o[...] = moment2
    for hop in (1, 2, 3):
        arrived, coming = coming, {}
        if hop == 3:
            opposite.wait_recv()
            pass_on(4)
        for k in range(2):
            for step in (1, 7):
                arrived[step, k].wait_recv()
                zz = at("z", hop * (8 - step))
                if hop < 3:
                    coming[step, k] = z_copy(upd.at[zz, xl, c, :, halves[k]], step)
                pass_on(hop * (8 - step), k)
        pass_core(4)
    pass_core(0)

    @pl.when(shard != z)
    def _():
        to_basis[0].wait_recv()

    for copy in last:
        copy.wait_recv()

    def out_columns(n, carry):
        here = pl.ds(pl.multiple_of(n * TILE, TILE), TILE)
        rows = jnp.concatenate(
            [upd[k // 4, (k // 2) % 2, k % 2, :, here] for k in range(32)], axis=0
        )
        change = jnp.dot(basis[...], rows, preferred_element_type=jnp.float32)
        w_o[:, here] = bf16(f32(weight[:, here]) - 0.2 * change)
        return carry

    lax.fori_loop(0, COLS // TILE, out_columns, 0)
    assert copies.count <= SEMS
    for copy in sent:
        copy.wait_send()
    for b in range(BLOCKS):

        @pl.when(st[b]["near"])
        def _():
            for group in (*st[b]["z"], st[b]["x"]):
                for copy in group:
                    copy.wait_send()

        @pl.when(jnp.logical_not(st[b]["near"]))
        def _():
            for copy in st[b]["core"]:
                copy.wait_send()

    @pl.when(shard == z)
    def _():
        for copy in to_basis:
            copy.wait_send()


SEMS = 256


def step(acts, grad_out, projector, weight, moment1, moment2):
    hbm = pl.BlockSpec(memory_space=pltpu.MemorySpace.HBM)
    half, full = jnp.bfloat16, jnp.float32
    pieces = (RANKS, PIECE)
    owned = (ROWS, COLS)
    scratch = [
        pltpu.VMEM(acts.shape, half),
        pltpu.VMEM(grad_out.shape, half),
        pltpu.VMEM(projector.shape, half),
        pltpu.VMEM(projector.shape, half),
        pltpu.VMEM(weight.shape, half),
        pltpu.VMEM(owned, full),
        pltpu.VMEM(owned, full),
        pltpu.VMEM((BLOCKS, 4, 2, *pieces), half),
        pltpu.VMEM((BLOCKS, 3, 2, *pieces), half),
        pltpu.VMEM((BLOCKS, *pieces), half),
        pltpu.VMEM((BLOCKS, *pieces), half),
        pltpu.VMEM((BLOCKS, 2, 4, *pieces), half),
        pltpu.VMEM((BLOCKS, 4, *pieces), half),
        pltpu.VMEM((BLOCKS, 3, *pieces), half),
        pltpu.VMEM((BLOCKS, 3, *pieces), half),
        pltpu.VMEM((2, BLOCKS * 8, *pieces), half),
        pltpu.VMEM((2, RANKS, COLS), full),
        pltpu.VMEM((BLOCKS, 8, *owned), half),
        pltpu.VMEM((BLOCKS, 8, *owned), half),
        pltpu.VMEM((2, 8, *owned), half),
        pltpu.VMEM((2, *owned), full),
        pltpu.VMEM((2, 7, *owned), half),
        pltpu.VMEM((2, *owned), half),
        pltpu.VMEM((2, *owned), half),
        pltpu.VMEM((3, 8, 128), full),
        pltpu.VMEM((7, 8, 128), full),
        pltpu.VMEM((7, 8, 128), full),
        pltpu.VMEM((1, 8, 128), full),
        pltpu.VMEM((8, 2, 2, *owned), half),
        pltpu.VMEM((PIECE, R), half),
        pltpu.SemaphoreType.DMA((SEMS,)),
        pltpu.SemaphoreType.DMA((SEMS,)),
        pltpu.SemaphoreType.DMA((9,)),
    ]
    outs = (
        jax.ShapeDtypeStruct(weight.shape, half),
        jax.ShapeDtypeStruct(owned, full),
        jax.ShapeDtypeStruct(owned, full),
    )
    results = pl.pallas_call(
        kernel,
        out_shape=tuple(pltpu.VMEM(out.shape, out.dtype) for out in outs),
        in_specs=[hbm] * 6,
        out_specs=(pl.BlockSpec(memory_space=pltpu.MemorySpace.VMEM),) * 3,
        scratch_shapes=scratch,
        name="galore_step",
        compiler_params=pltpu.CompilerParams(
            collective_id=0, has_side_effects=True, vmem_limit_bytes=48 << 20
        ),
    )(acts, grad_out, projector, weight, moment1, moment2)
    return results


def solution(mesh):
    finer = Mesh(mesh.devices.reshape(8, 2, 2, 4, 2), ("z", "xl", "c", "y", "xh"))
    dp, shard = ("z", "xl", "c"), ("y", "xh")
    both = P(dp, shard)
    return jax.shard_map(
        step,
        mesh=finer,
        in_specs=(both, both, P(shard, None), both, both, both),
        out_specs=(both, both, both),
        check_vma=False,
    )
```

```python
import functools

import jax
import jax.numpy as jnp
from jax import lax
from jax.experimental import pallas as pl
from jax.experimental.pallas import tpu as pltpu
from jax.sharding import Mesh
from jax.sharding import PartitionSpec as P

MESH = pl.DeviceIdType.MESH
TOKENS = 2048
FEATS = 512
R = 512
COLS = 1792
FF = 14336
BLOCKS = 4
RANKS = R // BLOCKS
PIECE = 128
ROWS = 16
TILE = 896
OFFSETS = dict(p=0, sx=5, sy=4.9, tx=8, ty=7.9, fy=12, fx=11.9, m=16, n=16.1, o=16.2, z=19, x=27)
PERIOD = 3
ORDER = [
    (name, b)
    for _, b, name in sorted(
        (b * PERIOD + offset, b, name) for b in range(BLOCKS) for name, offset in OFFSETS.items()
    )
]
FIRST_PRODUCT = next(item for item in ORDER if item[0] == "m")
SIZES = {"z": 8, "xl": 2, "c": 2, "y": 4, "xh": 2}
FAR_FIRST = (4, 3, 5, 2, 6, 1, 7)

first_fix = 0.9999734386011124
second_fix = 0.994079470779666


def f32(x):
    return x.astype(jnp.float32)


def bf16(x):
    return x.astype(jnp.bfloat16)


class Copies:
    def __init__(self, send_sems, recv_sems):
        self.send_sems, self.recv_sems, self.count = send_sems, recv_sems, 0

    def next(self):
        self.count += 1
        return self.count - 1

    def make(self, src, dst, recv=None, **device):
        k = self.next()
        return pltpu.make_async_remote_copy(
            src_ref=src,
            dst_ref=dst,
            send_sem=self.send_sems.at[k],
            recv_sem=self.recv_sems.at[k if recv is None else recv],
            device_id=device,
            device_id_type=MESH,
        )


def kernel(
    acts_h, grad_h, proj_h, weight_h, m1_h, m2_h,
    w_o, m1_o, m2_o,
    acts, grad, proj, proj_t, weight, m1, m2,
    s1, r1, x1s, x1r, s2, r2, y2s, y2r, full,
    mine, core_s, core_r, z_s, z_own, z_r, x_s, x_r,
    sq, sq_z, sq_s, sq_c, upd, basis,
    send_sems, recv_sems, local_sems,
):
    z, xl, c = lax.axis_index("z"), lax.axis_index("xl"), lax.axis_index("c")
    y, xh = lax.axis_index("y"), lax.axis_index("xh")
    shard = y * 2 + xh
    me = {"z": z, "xl": xl, "c": c, "y": y, "xh": xh}

    def at(axis, step):
        return lax.rem(me[axis] + step, SIZES[axis])

    def shard_at(step):
        other = lax.rem(shard + step, 8)
        return {"y": lax.div(other, 2), "xh": lax.rem(other, 2)}

    loads = {}
    for k, (name, src, dst) in enumerate(
        (
            ("proj", proj_h, proj),
            ("acts", acts_h, acts),
            ("grad", grad_h, grad),
            ("m1", m1_h, m1),
            ("m2", m2_h, m2),
            ("weight", weight_h, weight),
        )
    ):
        loads[name] = pltpu.make_async_copy(src, dst, local_sems.at[k])
    loads["proj"].start()
    loads["acts"].start()

    partners = [{"z": at("z", d)} for d in range(1, 8)]
    partners += [shard_at(d) for d in range(1, 8)]
    partners += [{"c": 1 - c}, {"xl": 1 - xl}]
    barrier = pltpu.get_barrier_semaphore()
    for partner in partners:
        pl.semaphore_signal(barrier, inc=1, device_id=partner, device_id_type=MESH)

    loads["proj"].wait()
    proj_t[...] = proj[...].T
    loads["acts"].wait()
    for name in ("grad", "m1", "m2", "weight"):
        loads[name].start()

    copies = Copies(send_sems, recv_sems)
    sent = []

    def start(copy):
        copy.start()
        sent.append(copy)
        return copy

    def ranks_of(b):
        return jnp.concatenate(
            [proj_t[pl.ds(64 * k + ROWS * b, ROWS), :] for k in range(8)], axis=0
        )

    def project(lhs, token, count):
        rows = acts[pl.ds(pl.multiple_of(token, PIECE), count), :]
        return bf16(
            lax.dot_general(
                lhs, rows, (((1,), (1,)), ((), ())), preferred_element_type=jnp.float32
            )
        )

    st = [dict() for _ in range(BLOCKS)]

    def project_block(b):
        lhs = ranks_of(b)

        def x_half(h):
            token = 1024 + lax.rem(xh + h, 2) * 512
            out = project(lhs, token, 512)
            for k in range(4):
                s2[b, h, k] = out[:, k * PIECE : (k + 1) * PIECE]

        def y_quarter(d):
            out = project(lhs, at("y", d) * 256, 256)
            for k in range(2):
                s1[b, d, k] = out[:, k * PIECE : (k + 1) * PIECE]

        x_half(1)
        if b == ORDER[0][1]:
            pl.semaphore_wait(barrier, len(partners))
        st[b]["r2"] = start(copies.make(s2.at[b, 1], r2.at[b], xh=1 - xh))
        y_quarter(2)
        st[b]["r1"] = [start(copies.make(s1.at[b, 2], r1.at[b, 2], y=at("y", 2)))]
        for k, d in enumerate((1, 3)):
            y_quarter(d)
            st[b]["r1"].append(start(copies.make(s1.at[b, d], r1.at[b, k], y=at("y", d))))
        x_half(0)
        y_quarter(0)

    def sum1(b, half):
        value = f32(s1[b, 0, half])
        for k in range(3):
            value += f32(r1[b, k, half])
        return value

    def second_x(b):
        for copy in st[b]["r1"]:
            copy.wait_recv()
        x1s[b] = bf16(sum1(b, 1 - xh))
        st[b]["x1"] = start(copies.make(x1s.at[b], x1r.at[b], xh=1 - xh))

    def second_y(b):
        st[b]["r2"].wait_recv()
        st[b]["y2"] = []
        for d in (2, 1, 3):
            other = at("y", d)
            y2s[b, d - 1] = bf16(f32(s2[b, 0, other]) + f32(r2[b, other]))
            st[b]["y2"].append(
                start(copies.make(y2s.at[b, d - 1], y2r.at[b, d - 1], y=other))
            )

    def third_x(b):
        st[b]["x1"].wait_recv()
        slot = 8 * b + y * 2 + xh
        full[0, slot] = bf16(sum1(b, xh) + f32(x1r[b]))
        st[b]["x3"] = start(copies.make(full.at[0, slot], full.at[0, slot], xh=1 - xh))

    def third_y(b):
        for copy in st[b]["y2"]:
            copy.wait_recv()
        value = f32(s2[b, 0, y]) + f32(r2[b, y])
        for k in range(3):
            value += f32(y2r[b, k])
        slot = 8 * b + xh * 4 + y
        full[1, slot] = bf16(value)
        st[b]["y3"] = [
            start(copies.make(full.at[1, slot], full.at[1, slot], y=at("y", d)))
            for d in (2, 1, 3)
        ]

    def fourth_y(b):
        st[b]["x3"].wait_recv()
        pair = full.at[0, pl.ds(8 * b + y * 2, 2)]
        st[b]["y4"] = [start(copies.make(pair, pair, y=at("y", d))) for d in (1, 3, 2)]

    def fourth_x(b):
        for copy in st[b]["y3"]:
            copy.wait_recv()
        four = full.at[1, pl.ds(8 * b + xh * 4, 4)]
        st[b]["x4"] = start(copies.make(four, four, xh=1 - xh))

    def parts(b):
        return ((0, 1), (1, 2)) if b == BLOCKS - 1 else ((0, 2),)

    def span_of(part):
        return pl.ds(part[0] * TILE, (part[1] - part[0]) * TILE)

    def arrived(b):
        for copy in st[b]["y4"]:
            copy.wait_recv()
        st[b]["x4"].wait_recv()
        st[b]["near"] = c == b % 2
        st[b]["core"] = []
        for part in parts(b):
            span = span_of(part)
            st[b]["core"].append(
                copies.make(core_s.at[b, :, :, span], core_r.at[b, :, :, span], c=1 - c)
            )

    def multiply(b, low, high):
        near = st[b]["near"]

        def columns(n, carry):
            here = pl.ds(pl.multiple_of(n * TILE, TILE), TILE)
            lhs = jnp.concatenate(
                [full[part, 8 * b + k] for part in range(2) for k in range(8)], axis=1
            )
            out = jnp.dot(lhs, grad[:, here], preferred_element_type=jnp.float32)

            @pl.when(near)
            def _():
                mine[b // 2, :, here] = out

            @pl.when(jnp.logical_not(near))
            def _():
                for k in range(8):
                    core_s[b, k, :, here] = bf16(out[k * ROWS : (k + 1) * ROWS])

            return carry

        lax.fori_loop(low, high, columns, 0)

    def multiply_0(b):
        arrived(b)
        pass

    def multiply_1(b):
        multiply(b, 0, 1)
        if len(parts(b)) > 1:
            pl.when(jnp.logical_not(st[b]["near"]))(st[b]["core"][0].start)

    def multiply_2(b):
        multiply(b, 1, 2)
        pl.when(jnp.logical_not(st[b]["near"]))(st[b]["core"][-1].start)

    def along_z(b):
        j = b // 2
        st[b]["z"] = []
        for part in parts(b):
            span = span_of(part)
            st[b]["z"].append(
                [
                    copies.make(
                        z_s.at[j, at("z", d), :, span], z_r.at[j, d - 1, :, span], z=at("z", d)
                    )
                    for d in FAR_FIRST
                ]
            )

        @pl.when(st[b]["near"])
        def _():
            for (low, high), core, group in zip(parts(b), st[b]["core"], st[b]["z"]):
                span = slice(low * TILE, high * TILE)
                core.wait_recv()
                for k in range(8):
                    z_s[j, k, :, span] = bf16(
                        mine[j, k * ROWS : (k + 1) * ROWS, span] + f32(core_r[b, k, :, span])
                    )
                for copy in group:
                    copy.start()
                own = pl.ds(pl.multiple_of(z * ROWS, ROWS), ROWS)
                z_own[j, :, span] = mine[j, own, span] + f32(core_r[b, z, :, span])

    def along_x(b):
        j = b // 2
        spans = [span_of(part) for part in parts(b)]
        st[b]["x"] = [
            copies.make(x_s.at[j, :, span], x_r.at[j, :, span], xl=1 - xl) for span in spans
        ]

        @pl.when(st[b]["near"])
        def _():
            for (low, high), group, copy in zip(parts(b), st[b]["z"], st[b]["x"]):
                span = slice(low * TILE, high * TILE)
                for arrived in group:
                    arrived.wait_recv()
                value = z_own[j, :, span]
                for k in range(7):
                    value += f32(z_r[j, k, :, span])
                z_own[j, :, span] = value
                x_s[j, :, span] = bf16(value)
                copy.start()

    offset = pl.multiple_of((xl * 2 + c) * PIECE, PIECE)
    rows = proj.at[pl.ds(offset, PIECE)]
    basis_sem = copies.next()
    to_basis = [copies.make(rows, basis, recv=basis_sem, **shard_at(d)) for d in range(1, 8)]

    def send_basis():
        @pl.when(shard == z)
        def _():
            for copy in to_basis:
                copy.start()
            basis[...] = proj[pl.ds(offset, PIECE), :]

    stages = {
        "p": project_block, "sx": second_x, "sy": second_y, "tx": third_x, "ty": third_y,
        "fy": fourth_y, "fx": fourth_x, "m": multiply_0, "n": multiply_1, "o": multiply_2,
        "z": along_z, "x": along_x,
    }
    for name, b in ORDER:
        if (name, b) == FIRST_PRODUCT:
            loads["grad"].wait()
        stages[name](b)
        if (name, b) == ("o", BLOCKS - 1):
            send_basis()

    for b in range(BLOCKS):

        @pl.when(st[b]["near"])
        def _():
            for copy in st[b]["x"]:
                copy.wait_recv()

    value = jnp.zeros((8, 128), jnp.float32)
    for j in range(2):
        gradient = z_own[j] + f32(x_r[j])
        z_own[j] = gradient
        square = gradient * gradient
        square = square[:8] + square[8:]
        for k in range(COLS // 128):
            value += square[:, k * 128 : (k + 1) * 128]

    def exchange(value, step, slots, partners):
        sq[step] = value
        arriving = [
            start(copies.make(sq.at[step], slots.at[k], **partner))
            for k, partner in enumerate(partners)
        ]
        for k, copy in enumerate(arriving):
            copy.wait_recv()
            value += slots[k]
        return value

    value = exchange(value, 0, sq_c, [{"c": 1 - c}])
    value = exchange(value, 1, sq_s, [shard_at(d) for d in range(1, 8)])
    value = exchange(value, 2, sq_z, [{"z": at("z", d)} for d in FAR_FIRST])
    root_mean = jnp.sqrt(jnp.sum(value, keepdims=True) / (R * FF) + 1e-06)
    clip_factor = jnp.minimum(1.0, 4.0 / root_mean)

    for name in ("m1", "m2", "weight"):
        loads[name].wait()
    clipped = clip_factor * z_own[xl]
    moment1 = 0.9 * m1[...] + 0.1 * clipped
    moment2 = 0.95 * m2[...] + 0.05 * clipped * clipped
    upd[z, xl, c] = bf16(moment1 / first_fix / (jnp.sqrt(moment2 / second_fix) + 1e-08))

    def piece(zz, xx):
        return upd.at[zz, xx, c]

    across, last = [], []

    def z_copy(part, step):
        return start(copies.make(part, part, z=at("z", step)))

    halves = [pl.ds(k * (COLS // 2), COLS // 2) for k in range(2)]

    def pass_on(step, k=None):
        zz = at("z", step)
        span = slice(None) if k is None else halves[k]
        part = upd.at[zz, xl, c, :, span]
        other = upd.at[zz, 1 - xl, c, :, span]
        across.append((start(copies.make(part, part, xl=1 - xl)), other))
        last.append(start(copies.make(part, part, c=1 - c)))

    def pass_core(keep):
        while len(across) > keep:
            copy, other = across.pop(0)
            copy.wait_recv()
            last.append(start(copies.make(other, other, c=1 - c)))

    coming = {}
    for k in range(2):
        for step in (1, 7):
            coming[step, k] = z_copy(upd.at[z, xl, c, :, halves[k]], step)
    opposite = z_copy(piece(z, xl), 4)
    pass_on(0)
    m1_o[...] = moment1
    m2_o[...] = moment2
    for hop in (1, 2, 3):
        arrived, coming = coming, {}
        if hop == 3:
            opposite.wait_recv()
            pass_on(4)
        for k in range(2):
            for step in (1, 7):
                arrived[step, k].wait_recv()
                zz = at("z", hop * (8 - step))
                if hop < 3:
                    coming[step, k] = z_copy(upd.at[zz, xl, c, :, halves[k]], step)
                pass_on(hop * (8 - step), k)
        pass_core(4)
    pass_core(0)

    @pl.when(shard != z)
    def _():
        to_basis[0].wait_recv()

    for copy in last:
        copy.wait_recv()

    def out_columns(n, carry):
        here = pl.ds(pl.multiple_of(n * TILE, TILE), TILE)
        rows = jnp.concatenate(
            [upd[k // 4, (k // 2) % 2, k % 2, :, here] for k in range(32)], axis=0
        )
        change = jnp.dot(basis[...], rows, preferred_element_type=jnp.float32)
        w_o[:, here] = bf16(f32(weight[:, here]) - 0.2 * change)
        return carry

    lax.fori_loop(0, COLS // TILE, out_columns, 0)
    assert copies.count <= SEMS
    for copy in sent:
        copy.wait_send()
    for b in range(BLOCKS):

        @pl.when(st[b]["near"])
        def _():
            for group in (*st[b]["z"], st[b]["x"]):
                for copy in group:
                    copy.wait_send()

        @pl.when(jnp.logical_not(st[b]["near"]))
        def _():
            for copy in st[b]["core"]:
                copy.wait_send()

    @pl.when(shard == z)
    def _():
        for copy in to_basis:
            copy.wait_send()


SEMS = 256


def step(acts, grad_out, projector, weight, moment1, moment2):
    hbm = pl.BlockSpec(memory_space=pltpu.MemorySpace.HBM)
    half, full = jnp.bfloat16, jnp.float32
    pieces = (RANKS, PIECE)
    owned = (ROWS, COLS)
    scratch = [
        pltpu.VMEM(acts.shape, half),
        pltpu.VMEM(grad_out.shape, half),
        pltpu.VMEM(projector.shape, half),
        pltpu.VMEM(projector.shape, half),
        pltpu.VMEM(weight.shape, half),
        pltpu.VMEM(owned, full),
        pltpu.VMEM(owned, full),
        pltpu.VMEM((BLOCKS, 4, 2, *pieces), half),
        pltpu.VMEM((BLOCKS, 3, 2, *pieces), half),
        pltpu.VMEM((BLOCKS, *pieces), half),
        pltpu.VMEM((BLOCKS, *pieces), half),
        pltpu.VMEM((BLOCKS, 2, 4, *pieces), half),
        pltpu.VMEM((BLOCKS, 4, *pieces), half),
        pltpu.VMEM((BLOCKS, 3, *pieces), half),
        pltpu.VMEM((BLOCKS, 3, *pieces), half),
        pltpu.VMEM((2, BLOCKS * 8, *pieces), half),
        pltpu.VMEM((2, RANKS, COLS), full),
        pltpu.VMEM((BLOCKS, 8, *owned), half),
        pltpu.VMEM((BLOCKS, 8, *owned), half),
        pltpu.VMEM((2, 8, *owned), half),
        pltpu.VMEM((2, *owned), full),
        pltpu.VMEM((2, 7, *owned), half),
        pltpu.VMEM((2, *owned), half),
        pltpu.VMEM((2, *owned), half),
        pltpu.VMEM((3, 8, 128), full),
        pltpu.VMEM((7, 8, 128), full),
        pltpu.VMEM((7, 8, 128), full),
        pltpu.VMEM((1, 8, 128), full),
        pltpu.VMEM((8, 2, 2, *owned), half),
        pltpu.VMEM((PIECE, R), half),
        pltpu.SemaphoreType.DMA((SEMS,)),
        pltpu.SemaphoreType.DMA((SEMS,)),
        pltpu.SemaphoreType.DMA((9,)),
    ]
    outs = (
        jax.ShapeDtypeStruct(weight.shape, half),
        jax.ShapeDtypeStruct(owned, full),
        jax.ShapeDtypeStruct(owned, full),
    )
    results = pl.pallas_call(
        kernel,
        out_shape=tuple(pltpu.VMEM(out.shape, out.dtype) for out in outs),
        in_specs=[hbm] * 6,
        out_specs=(pl.BlockSpec(memory_space=pltpu.MemorySpace.VMEM),) * 3,
        scratch_shapes=scratch,
        name="galore_step",
        compiler_params=pltpu.CompilerParams(
            collective_id=0, has_side_effects=True, vmem_limit_bytes=56 << 20
        ),
    )(acts, grad_out, projector, weight, moment1, moment2)
    return results


def solution(mesh):
    finer = Mesh(mesh.devices.reshape(8, 2, 2, 4, 2), ("z", "xl", "c", "y", "xh"))
    dp, shard = ("z", "xl", "c"), ("y", "xh")
    both = P(dp, shard)
    return jax.shard_map(
        step,
        mesh=finer,
        in_specs=(both, both, P(shard, None), both, both, both),
        out_specs=(both, both, both),
        check_vma=False,
    )
```

```python
import functools

import jax
import jax.numpy as jnp
from jax import lax
from jax.experimental import pallas as pl
from jax.experimental.pallas import tpu as pltpu
from jax.sharding import Mesh
from jax.sharding import PartitionSpec as P

MESH = pl.DeviceIdType.MESH
TOKENS = 2048
FEATS = 512
R = 512
COLS = 1792
FF = 14336
BLOCKS = 4
RANKS = R // BLOCKS
PIECE = 128
ROWS = 16
TILE = 896
OFFSETS = dict(p=0, sx=5, sy=4.9, tx=8, ty=7.9, fy=12, fx=11.9, m=16, n=16.1, o=16.2, z=19, x=27)
PERIOD = 3
ORDER = [
    (name, b)
    for _, b, name in sorted(
        (b * PERIOD + offset, b, name) for b in range(BLOCKS) for name, offset in OFFSETS.items()
    )
]
FIRST_PRODUCT = next(item for item in ORDER if item[0] == "m")
SIZES = {"z": 8, "xl": 2, "c": 2, "y": 4, "xh": 2}
FAR_FIRST = (4, 3, 5, 2, 6, 1, 7)

first_fix = 0.9999734386011124
second_fix = 0.994079470779666


def f32(x):
    return x.astype(jnp.float32)


def bf16(x):
    return x.astype(jnp.bfloat16)


class Copies:
    def __init__(self, send_sems, recv_sems):
        self.send_sems, self.recv_sems, self.count = send_sems, recv_sems, 0

    def next(self):
        self.count += 1
        return self.count - 1

    def make(self, src, dst, recv=None, **device):
        k = self.next()
        return pltpu.make_async_remote_copy(
            src_ref=src,
            dst_ref=dst,
            send_sem=self.send_sems.at[k],
            recv_sem=self.recv_sems.at[k if recv is None else recv],
            device_id=device,
            device_id_type=MESH,
        )


def kernel(
    acts_h, grad_h, proj_h, weight_h, m1_h, m2_h,
    w_o, m1_o, m2_o,
    acts, grad, proj, proj_t, weight, m1, m2,
    s1, r1, x1s, x1r, s2, r2, y2s, y2r, full,
    mine, core_s, core_r, z_s, z_own, z_r, x_s, x_r,
    sq, sq_z, sq_s, upd, basis,
    send_sems, recv_sems, local_sems,
):
    z, xl, c = lax.axis_index("z"), lax.axis_index("xl"), lax.axis_index("c")
    y, xh = lax.axis_index("y"), lax.axis_index("xh")
    shard = y * 2 + xh
    me = {"z": z, "xl": xl, "c": c, "y": y, "xh": xh}

    def at(axis, step):
        return lax.rem(me[axis] + step, SIZES[axis])

    def shard_at(step):
        other = lax.rem(shard + step, 8)
        return {"y": lax.div(other, 2), "xh": lax.rem(other, 2)}

    loads = {}
    for k, (name, src, dst) in enumerate(
        (
            ("proj", proj_h, proj),
            ("acts", acts_h, acts),
            ("grad", grad_h, grad),
            ("m1", m1_h, m1),
            ("m2", m2_h, m2),
            ("weight", weight_h, weight),
        )
    ):
        loads[name] = pltpu.make_async_copy(src, dst, local_sems.at[k])
    loads["proj"].start()
    loads["acts"].start()

    partners = [{"z": at("z", d)} for d in range(1, 8)]
    partners += [shard_at(d) for d in range(1, 8)]
    partners += [{"c": 1 - c}, {"xl": 1 - xl}]
    partners += [{"c": 1 - c, **shard_at(d)} for d in range(1, 8)]
    nearby = [shard_at(d) for d in range(1, 8)]
    nearby += [{"c": 1 - c, **device} for device in nearby] + [{"c": 1 - c}]
    barrier = pltpu.get_barrier_semaphore()
    for partner in partners:
        pl.semaphore_signal(barrier, inc=1, device_id=partner, device_id_type=MESH)

    loads["proj"].wait()
    proj_t[...] = proj[...].T
    loads["acts"].wait()
    for name in ("grad", "m1", "m2", "weight"):
        loads[name].start()

    copies = Copies(send_sems, recv_sems)
    sent = []

    def start(copy):
        copy.start()
        sent.append(copy)
        return copy

    def ranks_of(b):
        return jnp.concatenate(
            [proj_t[pl.ds(64 * k + ROWS * b, ROWS), :] for k in range(8)], axis=0
        )

    def project(lhs, token, count):
        rows = acts[pl.ds(pl.multiple_of(token, PIECE), count), :]
        return bf16(
            lax.dot_general(
                lhs, rows, (((1,), (1,)), ((), ())), preferred_element_type=jnp.float32
            )
        )

    st = [dict() for _ in range(BLOCKS)]

    def project_block(b):
        lhs = ranks_of(b)

        def x_half(h):
            token = 1024 + lax.rem(xh + h, 2) * 512
            out = project(lhs, token, 512)
            for k in range(4):
                s2[b, h, k] = out[:, k * PIECE : (k + 1) * PIECE]

        def y_quarter(d):
            out = project(lhs, at("y", d) * 256, 256)
            for k in range(2):
                s1[b, d, k] = out[:, k * PIECE : (k + 1) * PIECE]

        x_half(1)
        if b == ORDER[0][1]:
            pl.semaphore_wait(barrier, len(partners))
        st[b]["r2"] = start(copies.make(s2.at[b, 1], r2.at[b], xh=1 - xh))
        y_quarter(2)
        st[b]["r1"] = [start(copies.make(s1.at[b, 2], r1.at[b, 2], y=at("y", 2)))]
        for k, d in enumerate((1, 3)):
            y_quarter(d)
            st[b]["r1"].append(start(copies.make(s1.at[b, d], r1.at[b, k], y=at("y", d))))
        x_half(0)
        y_quarter(0)

    def sum1(b, half):
        value = f32(s1[b, 0, half])
        for k in range(3):
            value += f32(r1[b, k, half])
        return value

    def second_x(b):
        for copy in st[b]["r1"]:
            copy.wait_recv()
        x1s[b] = bf16(sum1(b, 1 - xh))
        st[b]["x1"] = start(copies.make(x1s.at[b], x1r.at[b], xh=1 - xh))

    def second_y(b):
        st[b]["r2"].wait_recv()
        st[b]["y2"] = []
        for d in (2, 1, 3):
            other = at("y", d)
            y2s[b, d - 1] = bf16(f32(s2[b, 0, other]) + f32(r2[b, other]))
            st[b]["y2"].append(
                start(copies.make(y2s.at[b, d - 1], y2r.at[b, d - 1], y=other))
            )

    def third_x(b):
        st[b]["x1"].wait_recv()
        slot = 8 * b + y * 2 + xh
        full[0, slot] = bf16(sum1(b, xh) + f32(x1r[b]))
        st[b]["x3"] = start(copies.make(full.at[0, slot], full.at[0, slot], xh=1 - xh))

    def third_y(b):
        for copy in st[b]["y2"]:
            copy.wait_recv()
        value = f32(s2[b, 0, y]) + f32(r2[b, y])
        for k in range(3):
            value += f32(y2r[b, k])
        slot = 8 * b + xh * 4 + y
        full[1, slot] = bf16(value)
        st[b]["y3"] = [
            start(copies.make(full.at[1, slot], full.at[1, slot], y=at("y", d)))
            for d in (2, 1, 3)
        ]

    def fourth_y(b):
        st[b]["x3"].wait_recv()
        pair = full.at[0, pl.ds(8 * b + y * 2, 2)]
        st[b]["y4"] = [start(copies.make(pair, pair, y=at("y", d))) for d in (1, 3, 2)]

    def fourth_x(b):
        for copy in st[b]["y3"]:
            copy.wait_recv()
        four = full.at[1, pl.ds(8 * b + xh * 4, 4)]
        st[b]["x4"] = start(copies.make(four, four, xh=1 - xh))

    def parts(b):
        return ((0, 1), (1, 2)) if b == BLOCKS - 1 else ((0, 2),)

    def span_of(part):
        return pl.ds(part[0] * TILE, (part[1] - part[0]) * TILE)

    def arrived(b):
        for copy in st[b]["y4"]:
            copy.wait_recv()
        st[b]["x4"].wait_recv()
        st[b]["near"] = c == b % 2
        st[b]["core"] = []
        for part in parts(b):
            span = span_of(part)
            st[b]["core"].append(
                copies.make(core_s.at[b, :, :, span], core_r.at[b, :, :, span], c=1 - c)
            )

    def multiply(b, low, high):
        near = st[b]["near"]

        def columns(n, carry):
            here = pl.ds(pl.multiple_of(n * TILE, TILE), TILE)
            lhs = jnp.concatenate(
                [full[part, 8 * b + k] for part in range(2) for k in range(8)], axis=1
            )
            out = jnp.dot(lhs, grad[:, here], preferred_element_type=jnp.float32)

            @pl.when(near)
            def _():
                mine[b // 2, :, here] = out

            @pl.when(jnp.logical_not(near))
            def _():
                for k in range(8):
                    core_s[b, k, :, here] = bf16(out[k * ROWS : (k + 1) * ROWS])

            return carry

        lax.fori_loop(low, high, columns, 0)

    def multiply_0(b):
        arrived(b)
        pass

    def multiply_1(b):
        multiply(b, 0, 1)
        if len(parts(b)) > 1:
            pl.when(jnp.logical_not(st[b]["near"]))(st[b]["core"][0].start)

    def multiply_2(b):
        multiply(b, 1, 2)
        pl.when(jnp.logical_not(st[b]["near"]))(st[b]["core"][-1].start)

    def along_z(b):
        j = b // 2
        st[b]["z"] = []
        for part in parts(b):
            span = span_of(part)
            st[b]["z"].append(
                [
                    copies.make(
                        z_s.at[j, at("z", d), :, span], z_r.at[j, d - 1, :, span], z=at("z", d)
                    )
                    for d in FAR_FIRST
                ]
            )

        @pl.when(st[b]["near"])
        def _():
            for (low, high), core, group in zip(parts(b), st[b]["core"], st[b]["z"]):
                span = slice(low * TILE, high * TILE)
                core.wait_recv()
                for k in range(8):
                    z_s[j, k, :, span] = bf16(
                        mine[j, k * ROWS : (k + 1) * ROWS, span] + f32(core_r[b, k, :, span])
                    )
                for copy in group:
                    copy.start()
                own = pl.ds(pl.multiple_of(z * ROWS, ROWS), ROWS)
                z_own[j, :, span] = mine[j, own, span] + f32(core_r[b, z, :, span])

    def along_x(b):
        j = b // 2
        spans = [span_of(part) for part in parts(b)]
        st[b]["x"] = [
            copies.make(x_s.at[j, :, span], x_r.at[j, :, span], xl=1 - xl) for span in spans
        ]

        @pl.when(st[b]["near"])
        def _():
            for (low, high), group, copy in zip(parts(b), st[b]["z"], st[b]["x"]):
                span = slice(low * TILE, high * TILE)
                for arrived in group:
                    arrived.wait_recv()
                value = z_own[j, :, span]
                for k in range(7):
                    value += f32(z_r[j, k, :, span])
                z_own[j, :, span] = value
                x_s[j, :, span] = bf16(value)
                copy.start()

    offset = pl.multiple_of((xl * 2 + c) * PIECE, PIECE)
    rows = proj.at[pl.ds(offset, PIECE)]
    basis_sem = copies.next()
    to_basis = [copies.make(rows, basis, recv=basis_sem, **shard_at(d)) for d in range(1, 8)]

    def send_basis():
        @pl.when(shard == z)
        def _():
            for copy in to_basis:
                copy.start()
            basis[...] = proj[pl.ds(offset, PIECE), :]

    stages = {
        "p": project_block, "sx": second_x, "sy": second_y, "tx": third_x, "ty": third_y,
        "fy": fourth_y, "fx": fourth_x, "m": multiply_0, "n": multiply_1, "o": multiply_2,
        "z": along_z, "x": along_x,
    }
    for name, b in ORDER:
        if (name, b) == FIRST_PRODUCT:
            loads["grad"].wait()
        stages[name](b)
        if (name, b) == ("o", BLOCKS - 1):
            send_basis()

    for b in range(BLOCKS):

        @pl.when(st[b]["near"])
        def _():
            for copy in st[b]["x"]:
                copy.wait_recv()

    value = jnp.zeros((8, 128), jnp.float32)
    for j in range(2):
        gradient = z_own[j] + f32(x_r[j])
        z_own[j] = gradient
        square = gradient * gradient
        square = square[:8] + square[8:]
        for k in range(COLS // 128):
            value += square[:, k * 128 : (k + 1) * 128]

    def exchange(value, step, slots, partners):
        sq[step] = value
        arriving = [
            start(copies.make(sq.at[step], slots.at[k], **partner))
            for k, partner in enumerate(partners)
        ]
        for k, copy in enumerate(arriving):
            copy.wait_recv()
            value += slots[k]
        return value

    value = exchange(value, 0, sq_s, nearby)
    value = exchange(value, 1, sq_z, [{"z": at("z", d)} for d in FAR_FIRST])
    root_mean = jnp.sqrt(jnp.sum(value, keepdims=True) / (R * FF) + 1e-06)
    clip_factor = jnp.minimum(1.0, 4.0 / root_mean)

    for name in ("m1", "m2", "weight"):
        loads[name].wait()
    clipped = clip_factor * z_own[xl]
    moment1 = 0.9 * m1[...] + 0.1 * clipped
    moment2 = 0.95 * m2[...] + 0.05 * clipped * clipped
    upd[z, xl, c] = bf16(moment1 / first_fix / (jnp.sqrt(moment2 / second_fix) + 1e-08))

    def piece(zz, xx):
        return upd.at[zz, xx, c]

    across, last = [], []

    def z_copy(part, step):
        return start(copies.make(part, part, z=at("z", step)))

    halves = [pl.ds(k * (COLS // 2), COLS // 2) for k in range(2)]

    def pass_on(step, k=None):
        zz = at("z", step)
        span = slice(None) if k is None else halves[k]
        part = upd.at[zz, xl, c, :, span]
        other = upd.at[zz, 1 - xl, c, :, span]
        across.append((start(copies.make(part, part, xl=1 - xl)), other))
        last.append(start(copies.make(part, part, c=1 - c)))

    def pass_core(keep):
        while len(across) > keep:
            copy, other = across.pop(0)
            copy.wait_recv()
            last.append(start(copies.make(other, other, c=1 - c)))

    coming = {}
    for k in range(2):
        for step in (1, 7):
            coming[step, k] = z_copy(upd.at[z, xl, c, :, halves[k]], step)
    opposite = z_copy(piece(z, xl), 4)
    pass_on(0)
    m1_o[...] = moment1
    m2_o[...] = moment2
    for hop in (1, 2, 3):
        arrived, coming = coming, {}
        if hop == 3:
            opposite.wait_recv()
            pass_on(4)
        for k in range(2):
            for step in (1, 7):
                arrived[step, k].wait_recv()
                zz = at("z", hop * (8 - step))
                if hop < 3:
                    coming[step, k] = z_copy(upd.at[zz, xl, c, :, halves[k]], step)
                pass_on(hop * (8 - step), k)
        pass_core(4)
    pass_core(0)

    @pl.when(shard != z)
    def _():
        to_basis[0].wait_recv()

    for copy in last:
        copy.wait_recv()

    def out_columns(n, carry):
        here = pl.ds(pl.multiple_of(n * TILE, TILE), TILE)
        rows = jnp.concatenate(
            [upd[k // 4, (k // 2) % 2, k % 2, :, here] for k in range(32)], axis=0
        )
        change = jnp.dot(basis[...], rows, preferred_element_type=jnp.float32)
        w_o[:, here] = bf16(f32(weight[:, here]) - 0.2 * change)
        return carry

    lax.fori_loop(0, COLS // TILE, out_columns, 0)
    assert copies.count <= SEMS
    for copy in sent:
        copy.wait_send()
    for b in range(BLOCKS):

        @pl.when(st[b]["near"])
        def _():
            for group in (*st[b]["z"], st[b]["x"]):
                for copy in group:
                    copy.wait_send()

        @pl.when(jnp.logical_not(st[b]["near"]))
        def _():
            for copy in st[b]["core"]:
                copy.wait_send()

    @pl.when(shard == z)
    def _():
        for copy in to_basis:
            copy.wait_send()


SEMS = 256


def step(acts, grad_out, projector, weight, moment1, moment2):
    hbm = pl.BlockSpec(memory_space=pltpu.MemorySpace.HBM)
    half, full = jnp.bfloat16, jnp.float32
    pieces = (RANKS, PIECE)
    owned = (ROWS, COLS)
    scratch = [
        pltpu.VMEM(acts.shape, half),
        pltpu.VMEM(grad_out.shape, half),
        pltpu.VMEM(projector.shape, half),
        pltpu.VMEM(projector.shape, half),
        pltpu.VMEM(weight.shape, half),
        pltpu.VMEM(owned, full),
        pltpu.VMEM(owned, full),
        pltpu.VMEM((BLOCKS, 4, 2, *pieces), half),
        pltpu.VMEM((BLOCKS, 3, 2, *pieces), half),
        pltpu.VMEM((BLOCKS, *pieces), half),
        pltpu.VMEM((BLOCKS, *pieces), half),
        pltpu.VMEM((BLOCKS, 2, 4, *pieces), half),
        pltpu.VMEM((BLOCKS, 4, *pieces), half),
        pltpu.VMEM((BLOCKS, 3, *pieces), half),
        pltpu.VMEM((BLOCKS, 3, *pieces), half),
        pltpu.VMEM((2, BLOCKS * 8, *pieces), half),
        pltpu.VMEM((2, RANKS, COLS), full),
        pltpu.VMEM((BLOCKS, 8, *owned), half),
        pltpu.VMEM((BLOCKS, 8, *owned), half),
        pltpu.VMEM((2, 8, *owned), half),
        pltpu.VMEM((2, *owned), full),
        pltpu.VMEM((2, 7, *owned), half),
        pltpu.VMEM((2, *owned), half),
        pltpu.VMEM((2, *owned), half),
        pltpu.VMEM((3, 8, 128), full),
        pltpu.VMEM((7, 8, 128), full),
        pltpu.VMEM((15, 8, 128), full),
        pltpu.VMEM((8, 2, 2, *owned), half),
        pltpu.VMEM((PIECE, R), half),
        pltpu.SemaphoreType.DMA((SEMS,)),
        pltpu.SemaphoreType.DMA((SEMS,)),
        pltpu.SemaphoreType.DMA((9,)),
    ]
    outs = (
        jax.ShapeDtypeStruct(weight.shape, half),
        jax.ShapeDtypeStruct(owned, full),
        jax.ShapeDtypeStruct(owned, full),
    )
    results = pl.pallas_call(
        kernel,
        out_shape=tuple(pltpu.VMEM(out.shape, out.dtype) for out in outs),
        in_specs=[hbm] * 6,
        out_specs=(pl.BlockSpec(memory_space=pltpu.MemorySpace.VMEM),) * 3,
        scratch_shapes=scratch,
        name="galore_step",
        compiler_params=pltpu.CompilerParams(
            collective_id=0, has_side_effects=True, vmem_limit_bytes=56 << 20
        ),
    )(acts, grad_out, projector, weight, moment1, moment2)
    return results


def solution(mesh):
    finer = Mesh(mesh.devices.reshape(8, 2, 2, 4, 2), ("z", "xl", "c", "y", "xh"))
    dp, shard = ("z", "xl", "c"), ("y", "xh")
    both = P(dp, shard)
    return jax.shard_map(
        step,
        mesh=finer,
        in_specs=(both, both, P(shard, None), both, both, both),
        out_specs=(both, both, both),
        check_vma=False,
    )
```
